32 devices in a mesh: band: 4 (over x, core), mem: 8 (over z, y).
Axes of the slice: x: 2, y: 2, z: 4, core: 2. Of those that a mesh axis runs over, the one named last changes fastest.
Arguments:
- members: bfloat16 [64, 16, 8192], P('band', None, 'mem'), may hold values from -6 to 6
- eigvecs: bfloat16 [112, 16, 8192], P('band', None, 'mem'), may hold values from -6 to 6
- control: float32 [112, 64], replicated, may hold values from -6 to 6
- columns: int32 [512, 16], P('mem'), may hold values from 0 to 1023
- interpolation: bfloat16 [512, 256, 512], P('mem'), may hold values from -0.375 to 0.375
- owners: int32 [512], replicated, may hold values from 0 to 7, as said below
- innovation: float32 [8, 256, 512], P('mem'), may hold values from -6 to 6
- obs_weight: float32 [8, 256, 512], P('mem'), may hold values from 0.25 to 4
Outputs:
- gradient: float32 [112, 64], P(None, 'band')
- departures: float32 [8, 256, 512], P('mem', None, 'band')
The draws below stay inside these ranges and needn't reach their ends.
Inputs may be any that keep to these rules, and one draw needn't show every extreme that they name: `owners`: one tile sends at most 32 of its blocks to one owner, and some owner holds exactly 32 blocks from every tile.
All inputs are finite; a program needn't handle non-finite values.
Results may differ from the reference program's by a relative error of at most 0.0032.
Values may be sent and summed in bfloat16 or wider, within the bound.
A program may use at most 64 MiB of HBM per device.

```python
import math
import jax
import jax.numpy as jnp
from jax import lax

MEMBERS = 64
MODES = 112
LEVELS = 16
PATCH = 16
OBS_BLOCK = 512
TILE_COLS = 1024
BLOCKS = 64
TILES = 8
GRID = 8192
CAPACITY = 32
SLOTS = 256


def draw_owners(key, part):
    base_key = jax.random.fold_in(key, 11)
    hot_key, shift_key, order_key = jax.random.split(base_key, 3)
    hottest = jax.random.randint(hot_key, (), 0, TILES)
    shifts = jax.random.randint(shift_key, (TILES,), 0, TILES - 1)
    places = jnp.arange(BLOCKS, dtype=jnp.int32)
    others = (places[None, :] - CAPACITY + shifts[:, None]) % (TILES - 1)
    chosen = jnp.where(places[None, :] < CAPACITY, hottest, (hottest + 1 + others) % TILES)
    tile_keys = jax.random.split(order_key, TILES)
    orders = jax.vmap(lambda k: jax.random.permutation(k, BLOCKS))(tile_keys)
    shuffled = jnp.take_along_axis(chosen, orders, axis=1)
    return shuffled.reshape(-1).astype(jnp.int32)


def plant(values, key, smallest, largest):
    place = [jax.random.randint(jax.random.fold_in(key, axis), (), 0, length) for axis, length in enumerate(values.shape)]
    main_axis = values.shape.index(max(values.shape))
    beside = place[:main_axis] + [(place[main_axis] + 1) % values.shape[main_axis]] + place[main_axis + 1:]
    return values.at[tuple(place)].set(smallest).at[tuple(beside)].set(largest)


def levels(key, dims, shards, least, top_value):
    def one(dim, blocks):
        heights = jax.random.uniform(jax.random.fold_in(jax.random.fold_in(key, 6), dim), (blocks,), jnp.float32, least / len(shards), top_value / len(shards))
        return jnp.repeat(jnp.exp(heights), dims[dim] // blocks).reshape((-1,) + (1,) * (len(dims) - dim - 1))

    level = one(*shards[0])
    for cut in shards[1:]:
        level = level * one(*cut)
    return level


def scatter_about(own_key, dims, deviation, reach, cuts=(), kind=jnp.bfloat16):
    loudness = levels(own_key, dims, cuts, -0.22, 0.18) if cuts else 1.0
    values = jax.random.normal(own_key, dims, jnp.float32) * deviation * loudness
    return jnp.minimum(jnp.maximum(values, -reach), reach).astype(kind)


def setup_inputs(seed: int = 0) -> dict:
    seeds = jax.random.split(jax.random.key(seed), 9)
    members = scatter_about(seeds[0], (MEMBERS, LEVELS, GRID), 1.0, 6.0, ((0, 4), (2, 8)))
    eigvecs = scatter_about(seeds[1], (MODES, LEVELS, GRID), 1.0, 6.0, ((0, 4), (2, 8)))
    control = scatter_about(seeds[2], (MODES, MEMBERS), 1.0, 6.0, (), jnp.float32)
    columns = plant(jax.random.randint(seeds[3], (TILES * BLOCKS, PATCH), 0, TILE_COLS), jax.random.fold_in(seeds[3], 1), 0, TILE_COLS - 1).astype(jnp.int32)
    interpolation = scatter_about(seeds[4], (TILES * BLOCKS, LEVELS * PATCH, OBS_BLOCK), (LEVELS * PATCH) ** -0.5, 0.375, ((0, 8),))
    owners = draw_owners(jax.random.fold_in(seeds[8], 71), 0)
    innovation = scatter_about(seeds[6], (TILES, SLOTS, OBS_BLOCK), 1.0, 6.0, ((0, 8),), jnp.float32)
    obs_weight = jnp.clip(jnp.exp(math.log(4.0) - 2.7725887 * jax.random.uniform(seeds[7], (TILES, SLOTS, OBS_BLOCK), jnp.float32) ** levels(seeds[7], (TILES, SLOTS, OBS_BLOCK), ((0, 8),), -0.2, 0.2)), 0.25, 4.0)
    return dict(members=members, eigvecs=eigvecs, control=control, columns=columns, interpolation=interpolation, owners=owners, innovation=innovation, obs_weight=obs_weight)


def tile_image(args):
    field, cols, blocks = args
    picked = field[:, cols.reshape(-1)].reshape(LEVELS, BLOCKS, PATCH)
    picked = jnp.transpose(picked, (1, 0, 2)).reshape(BLOCKS, LEVELS * PATCH)
    return jnp.einsum('jr,jro->jo', picked.astype(jnp.float32), blocks.astype(jnp.float32))

def tile_adjoint(args):
    cols, blocks, back = args
    spread = jnp.einsum('jro,jo->jr', blocks.astype(jnp.float32), back.astype(jnp.float32))
    spread = jnp.transpose(spread.reshape(BLOCKS, LEVELS, PATCH), (1, 0, 2)).reshape(LEVELS, BLOCKS * PATCH)
    return jnp.zeros((LEVELS, TILE_COLS), jnp.float32).at[:, cols.reshape(-1)].add(spread)

def reference(members, eigvecs, control, columns, interpolation, owners, innovation, obs_weight):
    scale = 1.0 / math.sqrt(MODES * MEMBERS)
    control_b = control.astype(jnp.bfloat16)
    mixed = jnp.dot(control_b.T, eigvecs.reshape(MODES, -1), preferred_element_type=jnp.float32)
    increment = scale * lax.optimization_barrier(jnp.sum(members.reshape(MEMBERS, -1).astype(jnp.float32) * mixed, axis=0))
    increment_b = increment.astype(jnp.bfloat16).reshape(LEVELS, TILES, TILE_COLS)
    col_tiles = columns.reshape(TILES, BLOCKS, PATCH)
    block_tiles = interpolation.reshape(TILES, BLOCKS, LEVELS * PATCH, OBS_BLOCK)
    image = lax.map(tile_image, (jnp.transpose(increment_b, (1, 0, 2)), col_tiles, block_tiles))
    own = owners.reshape(TILES, BLOCKS)
    order = jnp.arange(BLOCKS, dtype=jnp.int32)
    earlier = order[None, :] < order[:, None]
    same = own[:, :, None] == own[:, None, :]
    rank = lax.optimization_barrier(jnp.sum(jnp.logical_and(same, earlier[None]), axis=2)).astype(jnp.int32)
    slot = (jnp.arange(TILES, dtype=jnp.int32)[:, None] * CAPACITY + rank).astype(jnp.int32)
    slot_image = jnp.zeros((TILES, SLOTS, OBS_BLOCK), jnp.float32).at[own, slot].set(image)
    live = jnp.zeros((TILES, SLOTS), jnp.float32).at[own, slot].set(1.0)
    departures = live[:, :, None] * obs_weight * (innovation - slot_image)
    departures_b = departures.astype(jnp.bfloat16)
    back = departures_b[own, slot]
    adjoint = lax.map(tile_adjoint, (col_tiles, block_tiles, back))
    adjoint = jnp.transpose(adjoint, (1, 0, 2)).reshape(-1)
    weighted = (members.reshape(MEMBERS, -1).astype(jnp.float32) * adjoint).astype(jnp.bfloat16)
    total = jnp.dot(eigvecs.reshape(MODES, -1), weighted.T, preferred_element_type=jnp.float32)
    gradient = control - scale * total
    return (gradient, departures)
```

```python
import math

import jax
import jax.numpy as jnp
from jax import lax
from jax.sharding import PartitionSpec as P


def per_device(members, eigvecs, control, columns, interpolation, owners, innovation, obs_weight):
    nband = lax.axis_size("band")
    tiles = lax.axis_size("mem")
    band_idx = lax.axis_index("band")
    tile_idx = lax.axis_index("mem")
    mem_dev, levels, tile_cols = members.shape
    own_modes = eigvecs.shape[0]
    blocks, patch = columns.shape
    obs_block = interpolation.shape[2]
    capacity = innovation.shape[1] // tiles
    modes, total_members = control.shape
    scale = 1.0 / math.sqrt(modes * total_members)
    quarter = obs_block // nband
    eig_t = jnp.transpose(eigvecs, (1, 0, 2))
    all_members = lax.all_gather(jnp.transpose(members, (1, 0, 2)), "band", axis=1, tiled=True)
    weights = lax.dynamic_slice_in_dim(control, band_idx * own_modes, own_modes, 0)
    weights = jnp.broadcast_to(weights.astype(jnp.bfloat16)[None], (levels, own_modes, total_members))
    mixed = jnp.einsum("lkm,lkg->lmg", weights, eig_t, preferred_element_type=jnp.float32)
    partial_field = scale * jnp.sum(all_members * mixed, axis=1)
    increment_b = lax.psum(partial_field, "band").astype(jnp.bfloat16)
    selector = columns.reshape(-1)[:, None] == jnp.arange(tile_cols, dtype=jnp.int32)[None, :]
    picked = lax.dot_general(
        increment_b,
        selector.astype(jnp.bfloat16),
        (((1,), (1,)), ((), ())),
        preferred_element_type=jnp.float32,
    ).astype(jnp.bfloat16)
    picked = jnp.transpose(picked.reshape(levels, blocks, patch), (1, 0, 2)).reshape(
        blocks, levels * patch
    )
    interp = lax.dynamic_slice_in_dim(interpolation, band_idx * quarter, quarter, 2)
    innov_part = lax.dynamic_slice_in_dim(innovation[0], band_idx * quarter, quarter, 1)
    weight_part = lax.dynamic_slice_in_dim(obs_weight[0], band_idx * quarter, quarter, 1)
    image = jnp.einsum("jr,jro->jo", picked, interp, preferred_element_type=jnp.float32)
    local_owner = lax.dynamic_slice_in_dim(owners, tile_idx * blocks, blocks, 0)
    order = jnp.arange(blocks, dtype=jnp.int32)
    earlier = order[None, :] < order[:, None]
    same = local_owner[:, None] == local_owner[None, :]
    rank = jnp.sum(jnp.logical_and(same, earlier), axis=1)
    target = local_owner * capacity + rank
    placing = jnp.arange(tiles * capacity, dtype=jnp.int32)[:, None] == target[None, :]
    send = jnp.dot(placing.astype(jnp.float32), image, precision=lax.Precision.HIGHEST)
    arrived = lax.all_to_all(
        send.reshape(tiles, capacity, quarter), "mem", split_axis=0, concat_axis=0, tiled=True
    )
    arrived = arrived.reshape(tiles * capacity, quarter)
    counts = jnp.sum(owners.reshape(tiles, blocks) == tile_idx, axis=1)
    live = (jnp.arange(capacity)[None, :] < counts[:, None]).reshape(-1).astype(jnp.float32)
    departure = live[:, None] * weight_part * (innov_part - arrived)
    departure_b = departure.astype(jnp.bfloat16).reshape(tiles, capacity, quarter)
    returned = lax.all_to_all(departure_b, "mem", split_axis=0, concat_axis=0, tiled=True).reshape(
        tiles * capacity, quarter
    )
    own_back = jnp.dot(
        placing.T.astype(jnp.bfloat16), returned, preferred_element_type=jnp.float32
    ).astype(jnp.bfloat16)
    spread = jnp.einsum("jro,jo->jr", interp, own_back, preferred_element_type=jnp.float32)
    spread = jnp.transpose(spread.reshape(blocks, levels, patch), (1, 0, 2)).reshape(
        levels, blocks * patch
    )
    adjoint = jnp.dot(spread, selector.astype(jnp.float32), precision=lax.Precision.HIGHEST)
    adjoint = lax.psum(adjoint, "band")
    weighted = (all_members * adjoint[:, None, :]).astype(jnp.bfloat16)
    local_grad = jnp.einsum("lkg,lmg->km", eig_t, weighted, preferred_element_type=jnp.float32)
    turned = lax.all_to_all(local_grad, "band", split_axis=1, concat_axis=0, tiled=True)
    summed = lax.psum(turned, "mem")
    own_control = lax.dynamic_slice_in_dim(control, band_idx * mem_dev, mem_dev, 1)
    gradient = own_control - scale * summed
    return (gradient, departure[None])


def solution(mesh):
    return jax.shard_map(
        per_device,
        mesh=mesh,
        in_specs=(
            P("band", None, "mem"),
            P("band", None, "mem"),
            P(),
            P("mem", None),
            P("mem", None, None),
            P(),
            P("mem", None, None),
            P("mem", None, None),
        ),
        out_specs=(P(None, "band"), P("mem", None, "band")),
        check_vma=False,
    )
```

```python
import functools
import math

import jax
import jax.numpy as jnp
from jax import lax
from jax.experimental import pallas as pl
from jax.experimental.pallas import tpu as pltpu
from jax.sharding import PartitionSpec as P

MESH = pl.DeviceIdType.MESH
CHUNKS = 4
VMEM = pl.BlockSpec(memory_space=pltpu.VMEM)


def greet(axes):
    barrier = pltpu.get_barrier_semaphore()
    total = 0
    for axis, size in axes:
        me = lax.axis_index(axis)
        for step in range(1, size):
            pl.semaphore_signal(
                barrier, inc=1, device_id={axis: lax.rem(me + step, size)}, device_id_type=MESH
            )
        total += size - 1
    pl.semaphore_wait(barrier, total)


def remote(src, dst, send, recv, axis, peer):
    return pltpu.make_async_remote_copy(
        src_ref=src, dst_ref=dst, send_sem=send, recv_sem=recv,
        device_id={axis: peer}, device_id_type=MESH,
    )


def spread_part(parts, send, recv, index, rows, size):
    me = lax.axis_index("band")
    copies = []
    for step in range(1, size):
        block = parts.at[me, rows]
        copy = remote(
            block, block, send.at[index, step - 1], recv.at[index, step - 1],
            "band", lax.rem(me + step, size),
        )
        copy.start()
        copies.append(copy)
    return copies


def field_kernel(
    nband, scale, mem_ref, eig_ref, weight_ref, all_ref, inc_ref, mixed, parts,
    core_send, core_recv, far_send, far_recv, relay_send, relay_recv, part_send, part_recv, own_sem,
):
    me = lax.axis_index("band")
    levels, mem_dev, _ = mem_ref.shape
    each = levels // CHUNKS
    partner = me + 1 - 2 * lax.rem(me, 2)
    far = lax.rem(me + 2, nband)
    far_partner = lax.rem(partner + 2, nband)

    def place(band, rows):
        return all_ref.at[rows, pl.ds(pl.multiple_of(band * mem_dev, mem_dev), mem_dev)]

    greet((("band", nband),))
    chunks = [pl.ds(c * each, each) for c in range(CHUNKS)]
    far_copies = []
    for c, rows in enumerate(chunks):
        copy = remote(
            mem_ref.at[rows], place(me, rows), far_send.at[c], far_recv.at[c], "band", far
        )
        copy.start()
        far_copies.append(copy)
    whole = pl.ds(0, levels)
    core_copy = remote(mem_ref, place(me, whole), core_send, core_recv, "band", partner)
    core_copy.start()
    own_copy = pltpu.make_async_copy(mem_ref, place(me, whole), own_sem)
    own_copy.start()

    def mix(level, carry):
        mixed[level] = jnp.dot(
            weight_ref[...], eig_ref[level], preferred_element_type=jnp.float32
        )
        return carry

    lax.fori_loop(0, levels, mix, 0)
    own_copy.wait()
    core_copy.wait()
    relays = []

    def relay(c):
        far_copies[c].wait()
        copy = remote(
            place(far, chunks[c]), place(far, chunks[c]), relay_send.at[c], relay_recv.at[c],
            "band", partner,
        )
        copy.start()
        relays.append(copy)

    sends = []
    relay(0)
    for c, rows in enumerate(chunks):
        if c + 1 < CHUNKS:
            relay(c + 1)
        relays[c].wait()
        for i in range(each):
            level = c * each + i
            parts[me, level : level + 1] = jnp.sum(
                all_ref[level].astype(jnp.float32) * mixed[level], axis=0, keepdims=True
            )
        sends += spread_part(parts, part_send, part_recv, c, rows, nband)
    for copy in sends:
        copy.wait()
    total = parts[0]
    for band in range(1, nband):
        total = total + parts[band]
    inc_ref[...] = (scale * total).astype(inc_ref.dtype)


def exchange_kernel(
    tiles, send_ref, innov_ref, weight_ref, dep_ref, back_ref, arrived, rounded,
    out_send, out_recv, back_send, back_recv,
):
    me = lax.axis_index("mem")
    greet((("mem", tiles),))
    outs, backs = [], []
    for step in range(1, tiles):
        peer = lax.rem(me + step, tiles)
        copy = remote(
            send_ref.at[peer], arrived.at[me], out_send.at[step - 1], out_recv.at[step - 1],
            "mem", peer,
        )
        copy.start()
        outs.append(copy)
    own = weight_ref[me] * (innov_ref[me] - send_ref[me])
    dep_ref[me] = own
    back_ref[me] = own.astype(back_ref.dtype)
    for step in range(1, tiles):
        source = lax.rem(me + tiles - step, tiles)
        outs[step - 1].wait_recv()
        value = weight_ref[source] * (innov_ref[source] - arrived[source])
        dep_ref[source] = value
        rounded[source] = value.astype(rounded.dtype)
        copy = remote(
            rounded.at[source], back_ref.at[me], back_send.at[step - 1], back_recv.at[step - 1],
            "mem", source,
        )
        copy.start()
        backs.append(copy)
    for copy in outs:
        copy.wait_send()
    for copy in backs:
        copy.wait()


def gradient_kernel(
    nband, tiles, scale, adj_ref, all_ref, eig_ref, control_ref, grad_ref,
    parts, local, turned, sums,
    part_send, part_recv, turn_send, turn_recv, sum_send, sum_recv,
):
    band = lax.axis_index("band")
    tile = lax.axis_index("mem")
    levels = adj_ref.shape[0]
    each = levels // CHUNKS
    modes_dev = eig_ref.shape[1]
    mem_dev = local.shape[1]
    greet((("band", nband), ("mem", tiles)))
    parts[band] = adj_ref[...]
    sends = []
    for c in range(CHUNKS):
        sends.append(spread_part(parts, part_send, part_recv, c, pl.ds(c * each, each), nband))
    local[...] = jnp.zeros_like(local)
    total = None
    for c in range(CHUNKS):
        for copy in sends[c]:
            copy.wait()
        for i in range(each):
            level = c * each + i
            row = parts[0, level : level + 1]
            for b in range(1, nband):
                row = row + parts[b, level : level + 1]
            weighted = (all_ref[level].astype(jnp.float32) * row).astype(jnp.bfloat16)
            term = lax.dot_general(
                weighted, eig_ref[level], (((1,), (1,)), ((), ())),
                preferred_element_type=jnp.float32,
            )
            total = term if total is None else total + term
    for b in range(nband):
        local[b, :, :modes_dev] = total[b * mem_dev : (b + 1) * mem_dev]
    copies = []
    for step in range(1, nband):
        peer = lax.rem(band + step, nband)
        copy = remote(
            local.at[peer], turned.at[band], turn_send.at[step - 1], turn_recv.at[step - 1],
            "band", peer,
        )
        copy.start()
        copies.append(copy)
    turned[band] = local[band]
    for copy in copies:
        copy.wait()
    own = turned[0]
    for b in range(1, nband):
        own = own + pltpu.roll(turned[b], b * modes_dev, 1)
    sums[tile] = own
    copies = []
    for step in range(1, tiles):
        peer = lax.rem(tile + step, tiles)
        copy = remote(
            sums.at[tile], sums.at[tile], sum_send.at[step - 1], sum_recv.at[step - 1],
            "mem", peer,
        )
        copy.start()
        copies.append(copy)
    for copy in copies:
        copy.wait()
    whole = sums[0]
    for t in range(1, tiles):
        whole = whole + sums[t]
    grad_ref[...] = control_ref[...] - scale * whole[:, : grad_ref.shape[1]]


def dma(*shape):
    return pltpu.SemaphoreType.DMA(shape)


def params(collective_id):
    return pltpu.CompilerParams(
        collective_id=collective_id, has_side_effects=True, vmem_limit_bytes=40 << 20
    )


def per_device(members, eigvecs, control, columns, interpolation, owners, innovation, obs_weight):
    nband = lax.axis_size("band")
    tiles = lax.axis_size("mem")
    band_idx = lax.axis_index("band")
    tile_idx = lax.axis_index("mem")
    mem_dev, levels, tile_cols = members.shape
    own_modes = eigvecs.shape[0]
    blocks, patch = columns.shape
    obs_block = interpolation.shape[2]
    capacity = innovation.shape[1] // tiles
    modes, total_members = control.shape
    scale = 1.0 / math.sqrt(modes * total_members)
    quarter = obs_block // nband
    eig_t = jnp.transpose(eigvecs, (1, 0, 2))
    mem_t = jnp.transpose(members, (1, 0, 2))
    weights = lax.dynamic_slice_in_dim(control, band_idx * own_modes, own_modes, 0)
    weights = weights.astype(jnp.bfloat16).T
    all_members, increment_b = pl.pallas_call(
        functools.partial(field_kernel, nband, scale),
        out_shape=(
            jax.ShapeDtypeStruct((levels, total_members, tile_cols), jnp.bfloat16),
            jax.ShapeDtypeStruct((levels, tile_cols), jnp.bfloat16),
        ),
        in_specs=[VMEM] * 3,
        out_specs=(VMEM, VMEM),
        scratch_shapes=[
            pltpu.VMEM((levels, total_members, tile_cols), jnp.float32),
            pltpu.VMEM((nband, levels, tile_cols), jnp.float32),
            dma(), dma(), dma(CHUNKS), dma(CHUNKS), dma(CHUNKS), dma(CHUNKS),
            dma(CHUNKS, nband - 1), dma(CHUNKS, nband - 1), dma(),
        ],
        compiler_params=params(1),
    )(mem_t, eig_t, weights)
    selector = columns.reshape(-1)[:, None] == jnp.arange(tile_cols, dtype=jnp.int32)[None, :]
    picked = lax.dot_general(
        increment_b,
        selector.astype(jnp.bfloat16),
        (((1,), (1,)), ((), ())),
        preferred_element_type=jnp.float32,
    ).astype(jnp.bfloat16)
    picked = jnp.transpose(picked.reshape(levels, blocks, patch), (1, 0, 2)).reshape(
        blocks, levels * patch
    )
    interp = lax.dynamic_slice_in_dim(interpolation, band_idx * quarter, quarter, 2)
    innov_part = lax.dynamic_slice_in_dim(innovation[0], band_idx * quarter, quarter, 1)
    weight_part = lax.dynamic_slice_in_dim(obs_weight[0], band_idx * quarter, quarter, 1)
    image = jnp.einsum("jr,jro->jo", picked, interp, preferred_element_type=jnp.float32)
    local_owner = lax.dynamic_slice_in_dim(owners, tile_idx * blocks, blocks, 0)
    order = jnp.arange(blocks, dtype=jnp.int32)
    earlier = order[None, :] < order[:, None]
    same = local_owner[:, None] == local_owner[None, :]
    rank = jnp.sum(jnp.logical_and(same, earlier), axis=1)
    target = local_owner * capacity + rank
    placing = jnp.arange(tiles * capacity, dtype=jnp.int32)[:, None] == target[None, :]
    send = jnp.dot(placing.astype(jnp.float32), image, precision=lax.Precision.HIGHEST)
    counts = jnp.sum(owners.reshape(tiles, blocks) == tile_idx, axis=1)
    live = (jnp.arange(capacity)[None, :] < counts[:, None]).astype(jnp.float32)
    slots = (tiles, capacity, quarter)
    live_weight = live[:, :, None] * weight_part.reshape(slots)
    departure, returned = pl.pallas_call(
        functools.partial(exchange_kernel, tiles),
        out_shape=(
            jax.ShapeDtypeStruct(slots, jnp.float32),
            jax.ShapeDtypeStruct(slots, jnp.bfloat16),
        ),
        in_specs=[VMEM] * 3,
        out_specs=(VMEM, VMEM),
        scratch_shapes=[
            pltpu.VMEM(slots, jnp.float32), pltpu.VMEM(slots, jnp.bfloat16),
            dma(tiles - 1), dma(tiles - 1), dma(tiles - 1), dma(tiles - 1),
        ],
        compiler_params=params(2),
    )(send.reshape(slots), innov_part.reshape(slots), live_weight)
    departure = departure.reshape(tiles * capacity, quarter)
    returned = returned.reshape(tiles * capacity, quarter)
    own_back = jnp.dot(
        placing.T.astype(jnp.bfloat16), returned, preferred_element_type=jnp.float32
    ).astype(jnp.bfloat16)
    spread = jnp.einsum("jro,jo->jr", interp, own_back, preferred_element_type=jnp.float32)
    spread = jnp.transpose(spread.reshape(blocks, levels, patch), (1, 0, 2)).reshape(
        levels, blocks * patch
    )
    adjoint = jnp.dot(spread, selector.astype(jnp.float32), precision=lax.Precision.HIGHEST)
    own_control = lax.dynamic_slice_in_dim(control, band_idx * mem_dev, mem_dev, 1)
    lanes = pl.cdiv(modes, 128) * 128
    gradient = pl.pallas_call(
        functools.partial(gradient_kernel, nband, tiles, scale),
        out_shape=jax.ShapeDtypeStruct((mem_dev, modes), jnp.float32),
        in_specs=[VMEM] * 4,
        out_specs=VMEM,
        scratch_shapes=[
            pltpu.VMEM((nband, levels, tile_cols), jnp.float32),
            pltpu.VMEM((nband, mem_dev, lanes), jnp.float32),
            pltpu.VMEM((nband, mem_dev, lanes), jnp.float32),
            pltpu.VMEM((tiles, mem_dev, lanes), jnp.float32),
            dma(CHUNKS, nband - 1), dma(CHUNKS, nband - 1),
            dma(nband - 1), dma(nband - 1), dma(tiles - 1), dma(tiles - 1),
        ],
        compiler_params=params(3),
    )(adjoint, all_members, eig_t, own_control.T).T
    return (gradient, departure[None])


def solution(mesh):
    return jax.shard_map(
        per_device,
        mesh=mesh,
        in_specs=(
            P("band", None, "mem"),
            P("band", None, "mem"),
            P(),
            P("mem", None),
            P("mem", None, None),
            P(),
            P("mem", None, None),
            P("mem", None, None),
        ),
        out_specs=(P(None, "band"), P("mem", None, "band")),
        check_vma=False,
    )
```

```python
import functools
import math

import jax
import jax.numpy as jnp
from jax import lax
from jax.experimental import pallas as pl
from jax.experimental.pallas import tpu as pltpu
from jax.sharding import PartitionSpec as P

MESH = pl.DeviceIdType.MESH
CHUNKS = 4
VMEM = pl.BlockSpec(memory_space=pltpu.VMEM)


def greet(axes):
    barrier = pltpu.get_barrier_semaphore()
    total = 0
    for axis, size in axes:
        me = lax.axis_index(axis)
        for step in range(1, size):
            pl.semaphore_signal(
                barrier, inc=1, device_id={axis: lax.rem(me + step, size)}, device_id_type=MESH
            )
        total += size - 1
    pl.semaphore_wait(barrier, total)


def remote(src, dst, send, recv, axis, peer):
    return pltpu.make_async_remote_copy(
        src_ref=src, dst_ref=dst, send_sem=send, recv_sem=recv,
        device_id={axis: peer}, device_id_type=MESH,
    )


def spread_part(parts, send, recv, index, rows, size):
    me = lax.axis_index("band")
    copies = []
    for step in range(1, size):
        block = parts.at[me, rows]
        copy = remote(
            block, block, send.at[index, step - 1], recv.at[index, step - 1],
            "band", lax.rem(me + step, size),
        )
        copy.start()
        copies.append(copy)
    return copies


def split(value):
    high = value.astype(jnp.bfloat16)
    return high, (value - high.astype(jnp.float32)).astype(jnp.bfloat16)


def whole_kernel(
    nband, tiles, scale, mem_ref, eig_ref, weight_ref, cols_ref, target_ref, counts_ref,
    control_ref, interp_hbm, innov_hbm, obs_hbm, grad_ref, dep_ref,
    all_ref, mixed, parts, adj_parts, select, interp, innov, obs, image, spread, send, arrived,
    rounded, back, back_own, local, turned, sums,
    load_sem, core_send, core_recv, far_send, far_recv, relay_send, relay_recv,
    part_send, part_recv, out_send, out_recv, back_send, back_recv,
    adj_send, adj_recv, turn_send, turn_recv, sum_send, sum_recv,
):
    me = lax.axis_index("band")
    tile = lax.axis_index("mem")
    levels, mem_dev, tile_cols = mem_ref.shape
    modes_dev = eig_ref.shape[1]
    patch, blocks = cols_ref.shape
    capacity, quarter = send.shape[1:]
    each = levels // CHUNKS
    partner = me + 1 - 2 * lax.rem(me, 2)
    far = lax.rem(me + 2, nband)
    chunks = [pl.ds(c * each, each) for c in range(CHUNKS)]
    whole = pl.ds(0, levels)
    own_obs = pl.ds(pl.multiple_of(me * quarter, quarter), quarter)

    def place(band, rows):
        return all_ref.at[rows, pl.ds(pl.multiple_of(band * mem_dev, mem_dev), mem_dev)]

    own_copy = pltpu.make_async_copy(mem_ref, place(me, whole), load_sem.at[0])
    loads = [
        pltpu.make_async_copy(interp_hbm.at[:, :, own_obs], interp, load_sem.at[1]),
        pltpu.make_async_copy(innov_hbm.at[:, :, own_obs], innov, load_sem.at[2]),
        pltpu.make_async_copy(obs_hbm.at[:, :, own_obs], obs, load_sem.at[3]),
    ]
    greet((("band", nband), ("mem", tiles)))
    far_copies = []
    for c, rows in enumerate(chunks):
        copy = remote(
            mem_ref.at[rows], place(me, rows), far_send.at[c], far_recv.at[c], "band", far
        )
        copy.start()
        far_copies.append(copy)
    core_copy = remote(mem_ref, place(me, whole), core_send, core_recv, "band", partner)
    core_copy.start()
    own_copy.start()
    for copy in loads:
        copy.start()

    def mix(level, carry):
        mixed[level] = jnp.dot(
            weight_ref[...], eig_ref[level], preferred_element_type=jnp.float32
        )
        return carry

    lax.fori_loop(0, levels, mix, 0)
    column = lax.broadcasted_iota(jnp.int32, (patch, tile_cols), 1)
    for j in range(blocks):
        select[j * patch : (j + 1) * patch] = jnp.where(
            cols_ref[:, j : j + 1] == column, 1.0, 0.0
        ).astype(jnp.bfloat16)
    slot = lax.broadcasted_iota(jnp.int32, (tiles * capacity, blocks), 0)
    placing = jnp.where(slot == target_ref[...], 1.0, 0.0)
    own_copy.wait()
    core_copy.wait()
    relays = []

    def relay(c):
        far_copies[c].wait()
        copy = remote(
            place(far, chunks[c]), place(far, chunks[c]), relay_send.at[c], relay_recv.at[c],
            "band", partner,
        )
        copy.start()
        relays.append(copy)

    sends = []
    relay(0)
    for c, rows in enumerate(chunks):
        if c + 1 < CHUNKS:
            relay(c + 1)
        relays[c].wait()
        for i in range(each):
            level = c * each + i
            parts[me, level : level + 1] = jnp.sum(
                all_ref[level].astype(jnp.float32) * mixed[level], axis=0, keepdims=True
            )
        sends += spread_part(parts, part_send, part_recv, c, rows, nband)
    for copy in sends:
        copy.wait()
    total = parts[0]
    for band in range(1, nband):
        total = total + parts[band]
    increment = (scale * total).astype(jnp.bfloat16)

    spread[...] = lax.dot_general(
        select[...], increment, (((1,), (1,)), ((), ())), preferred_element_type=jnp.float32
    )
    for copy in loads:
        copy.wait()

    def project(j, carry):
        rows = pl.ds(pl.multiple_of(j * patch, patch), patch)
        value = spread[rows]
        total = jnp.zeros((patch, quarter), jnp.float32)
        for level in range(levels):
            total += value[:, level : level + 1] * interp[
                j, level * patch : (level + 1) * patch
            ].astype(jnp.float32)
        image[pl.ds(j, 1)] = jnp.sum(total, axis=0, keepdims=True)
        return carry

    lax.fori_loop(0, blocks, project, 0, unroll=2)
    send[...] = jnp.dot(
        placing, image[...], precision=lax.Precision.HIGHEST, preferred_element_type=jnp.float32
    ).reshape(send.shape)
    outs, backs = [], []
    for step in range(1, tiles):
        peer = lax.rem(tile + step, tiles)
        copy = remote(
            send.at[peer], arrived.at[tile], out_send.at[step - 1], out_recv.at[step - 1],
            "mem", peer,
        )
        copy.start()
        outs.append(copy)
    row = lax.broadcasted_iota(jnp.int32, (capacity, quarter), 0)

    def depart(source, value):
        rows = pl.ds(pl.multiple_of(source * capacity, capacity), capacity)
        live = jnp.where(row < counts_ref[source], 1.0, 0.0)
        result = live * obs[0, rows] * (innov[0, rows] - value)
        dep_ref[0, rows] = result
        return result.astype(jnp.bfloat16)

    back_own[...] = depart(tile, send[tile])
    for step in range(1, tiles):
        source = lax.rem(tile + tiles - step, tiles)
        outs[step - 1].wait_recv()
        rounded[source] = depart(source, arrived[source])
        copy = remote(
            rounded.at[source], back.at[tile], back_send.at[step - 1], back_recv.at[step - 1],
            "mem", source,
        )
        copy.start()
        backs.append(copy)
    back[tile] = back_own[...]
    for copy in outs:
        copy.wait_send()
    for copy in backs:
        copy.wait()
    image[...] = lax.dot_general(
        placing.astype(jnp.bfloat16), back[...].reshape(tiles * capacity, quarter),
        (((0,), (0,)), ((), ())), preferred_element_type=jnp.float32,
    )
    lane = lax.broadcasted_iota(jnp.int32, (patch, levels), 1)

    def gather_up(j, carry):
        own = jnp.broadcast_to(image[pl.ds(j, 1)], (levels, quarter)).astype(jnp.bfloat16)
        value = lax.dot_general(
            interp[j], own, (((1,), (1,)), ((), ())), preferred_element_type=jnp.float32
        )
        total = jnp.zeros((patch, levels), jnp.float32)
        for level in range(levels):
            total = jnp.where(lane == level, value[level * patch : (level + 1) * patch], total)
        spread[pl.ds(pl.multiple_of(j * patch, patch), patch)] = total
        return carry

    lax.fori_loop(0, blocks, gather_up, 0, unroll=4)
    high, low = split(spread[...])
    over = (((0,), (0,)), ((), ()))
    adj_parts[me] = lax.dot_general(
        high, select[...], over, preferred_element_type=jnp.float32
    ) + lax.dot_general(low, select[...], over, preferred_element_type=jnp.float32)
    sends = []
    for c, rows in enumerate(chunks):
        sends.append(spread_part(adj_parts, adj_send, adj_recv, c, rows, nband))
    local[...] = jnp.zeros_like(local)
    total = None
    for c in range(CHUNKS):
        for copy in sends[c]:
            copy.wait()
        for i in range(each):
            level = c * each + i
            adjoint = adj_parts[0, level : level + 1]
            for b in range(1, nband):
                adjoint = adjoint + adj_parts[b, level : level + 1]
            weighted = (all_ref[level].astype(jnp.float32) * adjoint).astype(jnp.bfloat16)
            term = lax.dot_general(
                weighted, eig_ref[level], (((1,), (1,)), ((), ())),
                preferred_element_type=jnp.float32,
            )
            total = term if total is None else total + term
    for b in range(nband):
        local[b, :, :modes_dev] = total[b * mem_dev : (b + 1) * mem_dev]
    copies = []
    for step in range(1, nband):
        peer = lax.rem(me + step, nband)
        copy = remote(
            local.at[peer], turned.at[me], turn_send.at[step - 1], turn_recv.at[step - 1],
            "band", peer,
        )
        copy.start()
        copies.append(copy)
    turned[me] = local[me]
    for copy in copies:
        copy.wait()
    own = turned[0]
    for b in range(1, nband):
        own = own + pltpu.roll(turned[b], b * modes_dev, 1)
    sums[tile] = own
    copies = []
    for step in range(1, tiles):
        peer = lax.rem(tile + step, tiles)
        copy = remote(
            sums.at[tile], sums.at[tile], sum_send.at[step - 1], sum_recv.at[step - 1],
            "mem", peer,
        )
        copy.start()
        copies.append(copy)
    for copy in copies:
        copy.wait()
    whole = sums[0]
    for t in range(1, tiles):
        whole = whole + sums[t]
    grad_ref[...] = control_ref[...] - scale * whole[:, : grad_ref.shape[1]]


def dma(*shape):
    return pltpu.SemaphoreType.DMA(shape)


def per_device(members, eigvecs, control, columns, interpolation, owners, innovation, obs_weight):
    nband = lax.axis_size("band")
    tiles = lax.axis_size("mem")
    band_idx = lax.axis_index("band")
    tile_idx = lax.axis_index("mem")
    mem_dev, levels, tile_cols = members.shape
    own_modes = eigvecs.shape[0]
    blocks, patch = columns.shape
    obs_block = interpolation.shape[2]
    capacity = innovation.shape[1] // tiles
    modes, total_members = control.shape
    scale = 1.0 / math.sqrt(modes * total_members)
    quarter = obs_block // nband
    eig_t = jnp.transpose(eigvecs, (1, 0, 2))
    mem_t = jnp.transpose(members, (1, 0, 2))
    weights = lax.dynamic_slice_in_dim(control, band_idx * own_modes, own_modes, 0)
    weights = weights.astype(jnp.bfloat16).T
    local_owner = lax.dynamic_slice_in_dim(owners, tile_idx * blocks, blocks, 0)
    order = jnp.arange(blocks, dtype=jnp.int32)
    earlier = order[None, :] < order[:, None]
    same = local_owner[:, None] == local_owner[None, :]
    rank = jnp.sum(jnp.logical_and(same, earlier), axis=1)
    target = (local_owner * capacity + rank)[None, :]
    counts = jnp.sum(owners.reshape(tiles, blocks) == tile_idx, axis=1)
    counts = jnp.broadcast_to(counts[:, None, None], (tiles, 1, quarter))
    own_control = lax.dynamic_slice_in_dim(control, band_idx * mem_dev, mem_dev, 1)
    lanes = pl.cdiv(modes, 128) * 128
    slots = (tiles, capacity, quarter)
    own_slots = (1, tiles * capacity, quarter)
    hbm = pl.BlockSpec(memory_space=pltpu.HBM)
    f32, bf16 = jnp.float32, jnp.bfloat16
    gradient, departure = pl.pallas_call(
        functools.partial(whole_kernel, nband, tiles, scale),
        out_shape=(
            jax.ShapeDtypeStruct((mem_dev, modes), f32),
            jax.ShapeDtypeStruct(own_slots, f32),
        ),
        in_specs=[VMEM] * 7 + [hbm] * 3,
        out_specs=(VMEM, VMEM),
        scratch_shapes=[
            pltpu.VMEM((levels, total_members, tile_cols), bf16),
            pltpu.VMEM((levels, total_members, tile_cols), f32),
            pltpu.VMEM((nband, levels, tile_cols), f32),
            pltpu.VMEM((nband, levels, tile_cols), f32),
            pltpu.VMEM((blocks * patch, tile_cols), bf16),
            pltpu.VMEM((blocks, levels * patch, quarter), bf16),
            pltpu.VMEM(own_slots, f32),
            pltpu.VMEM(own_slots, f32),
            pltpu.VMEM((blocks, quarter), f32),
            pltpu.VMEM((blocks * patch, levels), f32),
            pltpu.VMEM(slots, f32),
            pltpu.VMEM(slots, f32),
            pltpu.VMEM(slots, bf16),
            pltpu.VMEM(slots, bf16),
            pltpu.VMEM((capacity, quarter), bf16),
            pltpu.VMEM((nband, mem_dev, lanes), f32),
            pltpu.VMEM((nband, mem_dev, lanes), f32),
            pltpu.VMEM((tiles, mem_dev, lanes), f32),
            dma(4), dma(), dma(), dma(CHUNKS), dma(CHUNKS), dma(CHUNKS), dma(CHUNKS),
            dma(CHUNKS, nband - 1), dma(CHUNKS, nband - 1),
            dma(tiles - 1), dma(tiles - 1), dma(tiles - 1), dma(tiles - 1),
            dma(CHUNKS, nband - 1), dma(CHUNKS, nband - 1),
            dma(nband - 1), dma(nband - 1), dma(tiles - 1), dma(tiles - 1),
        ],
        compiler_params=pltpu.CompilerParams(
            collective_id=1, has_side_effects=True, vmem_limit_bytes=40 << 20
        ),
    )(
        mem_t, eig_t, weights, columns.T, target, counts, own_control.T,
        interpolation, innovation, obs_weight,
    )
    return (gradient.T, departure)


def solution(mesh):
    return jax.shard_map(
        per_device,
        mesh=mesh,
        in_specs=(
            P("band", None, "mem"),
            P("band", None, "mem"),
            P(),
            P("mem", None),
            P("mem", None, None),
            P(),
            P("mem", None, None),
            P("mem", None, None),
        ),
        out_specs=(P(None, "band"), P("mem", None, "band")),
        check_vma=False,
    )
```

```python
import functools
import math

import jax
import jax.numpy as jnp
from jax import lax
from jax.experimental import pallas as pl
from jax.experimental.pallas import tpu as pltpu
from jax.sharding import PartitionSpec as P

MESH = pl.DeviceIdType.MESH
CHUNKS = 4
VMEM = pl.BlockSpec(memory_space=pltpu.VMEM)


def greet(axes):
    barrier = pltpu.get_barrier_semaphore()
    total = 0
    for axis, size in axes:
        me = lax.axis_index(axis)
        for step in range(1, size):
            pl.semaphore_signal(
                barrier, inc=1, device_id={axis: lax.rem(me + step, size)}, device_id_type=MESH
            )
        total += size - 1
    pl.semaphore_wait(barrier, total)


def remote(src, dst, send, recv, axis, peer):
    return pltpu.make_async_remote_copy(
        src_ref=src, dst_ref=dst, send_sem=send, recv_sem=recv,
        device_id={axis: peer}, device_id_type=MESH,
    )


def spread_part(parts, send, recv, index, rows, size):
    me = lax.axis_index("band")
    copies = []
    for step in range(1, size):
        block = parts.at[me, rows]
        copy = remote(
            block, block, send.at[index, step - 1], recv.at[index, step - 1],
            "band", lax.rem(me + step, size),
        )
        copy.start()
        copies.append(copy)
    return copies


def split(value):
    high = value.astype(jnp.bfloat16)
    return high, (value - high.astype(jnp.float32)).astype(jnp.bfloat16)


def whole_kernel(
    nband, tiles, scale, mem_ref, eig_ref, weight_ref, cols_ref, owners_ref,
    control_ref, interp_hbm, innov_hbm, obs_hbm, grad_ref, dep_ref,
    all_ref, mixed, parts, adj_parts, select, interp, innov, obs, image, spread, send, arrived,
    rounded, back, back_own, local, turned, sums,
    load_sem, core_send, core_recv, far_send, far_recv, relay_send, relay_recv,
    part_send, part_recv, out_send, out_recv, back_send, back_recv,
    adj_send, adj_recv, turn_send, turn_recv, sum_send, sum_recv,
):
    me = lax.axis_index("band")
    tile = lax.axis_index("mem")
    levels, mem_dev, tile_cols = mem_ref.shape
    modes_dev = eig_ref.shape[1]
    patch, blocks = cols_ref.shape
    capacity, quarter = send.shape[1:]
    each = levels // CHUNKS
    partner = me + 1 - 2 * lax.rem(me, 2)
    far = lax.rem(me + 2, nband)
    chunks = [pl.ds(c * each, each) for c in range(CHUNKS)]
    whole = pl.ds(0, levels)
    own_obs = pl.ds(pl.multiple_of(me * quarter, quarter), quarter)

    def place(band, rows):
        return all_ref.at[rows, pl.ds(pl.multiple_of(band * mem_dev, mem_dev), mem_dev)]

    own_copy = pltpu.make_async_copy(mem_ref, place(me, whole), load_sem.at[0])
    loads = [
        pltpu.make_async_copy(interp_hbm.at[:, :, own_obs], interp, load_sem.at[1]),
        pltpu.make_async_copy(innov_hbm.at[:, :, own_obs], innov, load_sem.at[2]),
        pltpu.make_async_copy(obs_hbm.at[:, :, own_obs], obs, load_sem.at[3]),
    ]
    greet((("band", nband), ("mem", tiles)))
    far_copies = []
    for c, rows in enumerate(chunks):
        copy = remote(
            mem_ref.at[rows], place(me, rows), far_send.at[c], far_recv.at[c], "band", far
        )
        copy.start()
        far_copies.append(copy)
    core_copy = remote(mem_ref, place(me, whole), core_send, core_recv, "band", partner)
    core_copy.start()
    own_copy.start()
    for copy in loads:
        copy.start()

    def mix(level, carry):
        mixed[level] = jnp.dot(
            weight_ref[...], eig_ref[level], preferred_element_type=jnp.float32
        )
        return carry

    lax.fori_loop(0, levels, mix, 0)
    column = lax.broadcasted_iota(jnp.int32, (patch, tile_cols), 1)
    for j in range(blocks):
        select[j * patch : (j + 1) * patch] = jnp.where(
            cols_ref[:, j : j + 1] == column, 1.0, 0.0
        ).astype(jnp.bfloat16)
    owner = owners_ref[pl.ds(tile, 1)].astype(jnp.float32)
    down = lax.broadcasted_iota(jnp.int32, (blocks, blocks), 0)
    across = lax.broadcasted_iota(jnp.int32, (blocks, blocks), 1)
    owner_column = jnp.sum(jnp.where(down == across, owner, 0.0), axis=1, keepdims=True)
    same = jnp.where(jnp.logical_and(owner_column == owner, down < across), 1.0, 0.0)
    rank = jnp.sum(same, axis=0, keepdims=True)
    target = (owner * capacity + rank).astype(jnp.int32)
    slot = lax.broadcasted_iota(jnp.int32, (tiles * capacity, blocks), 0)
    placing = jnp.where(slot == target, 1.0, 0.0)
    counts = jnp.sum(
        jnp.where(owners_ref[...] == tile, 1.0, 0.0), axis=1, keepdims=True
    ).astype(jnp.int32)
    for copy in loads:
        copy.wait()
    row = lax.broadcasted_iota(jnp.int32, (capacity, quarter), 0)
    for t in range(tiles):
        rows = slice(t * capacity, (t + 1) * capacity)
        obs[0, rows] = jnp.where(row < counts[t : t + 1], 1.0, 0.0) * obs[0, rows]
    own_copy.wait()
    core_copy.wait()
    relays = []

    def relay(c):
        far_copies[c].wait()
        copy = remote(
            place(far, chunks[c]), place(far, chunks[c]), relay_send.at[c], relay_recv.at[c],
            "band", partner,
        )
        copy.start()
        relays.append(copy)

    sends = []
    relay(0)
    for c, rows in enumerate(chunks):
        if c + 1 < CHUNKS:
            relay(c + 1)
        relays[c].wait()
        for i in range(each):
            level = c * each + i
            parts[me, level : level + 1] = jnp.sum(
                all_ref[level].astype(jnp.float32) * mixed[level], axis=0, keepdims=True
            )
        sends += spread_part(parts, part_send, part_recv, c, rows, nband)
    for copy in sends:
        copy.wait()
    total = parts[0]
    for band in range(1, nband):
        total = total + parts[band]
    increment = (scale * total).astype(jnp.bfloat16)

    spread[...] = lax.dot_general(
        select[...], increment, (((1,), (1,)), ((), ())), preferred_element_type=jnp.float32
    )

    def project(j, carry):
        rows = pl.ds(pl.multiple_of(j * patch, patch), patch)
        value = spread[rows]
        total = jnp.zeros((patch, quarter), jnp.float32)
        for level in range(levels):
            total += value[:, level : level + 1] * interp[
                j, level * patch : (level + 1) * patch
            ].astype(jnp.float32)
        image[pl.ds(j, 1)] = jnp.sum(total, axis=0, keepdims=True)
        return carry

    lax.fori_loop(0, blocks, project, 0, unroll=4)
    send[...] = jnp.dot(
        placing, image[...], precision=lax.Precision.HIGHEST, preferred_element_type=jnp.float32
    ).reshape(send.shape)
    outs, backs = [], []
    for step in range(1, tiles):
        peer = lax.rem(tile + step, tiles)
        copy = remote(
            send.at[peer], arrived.at[tile], out_send.at[step - 1], out_recv.at[step - 1],
            "mem", peer,
        )
        copy.start()
        outs.append(copy)

    def depart(source, value):
        rows = pl.ds(pl.multiple_of(source * capacity, capacity), capacity)
        result = obs[0, rows] * (innov[0, rows] - value)
        dep_ref[0, rows] = result
        return result.astype(jnp.bfloat16)

    back_own[...] = depart(tile, send[tile])
    for step in range(1, tiles):
        source = lax.rem(tile + tiles - step, tiles)
        outs[step - 1].wait_recv()
        rounded[source] = depart(source, arrived[source])
        copy = remote(
            rounded.at[source], back.at[tile], back_send.at[step - 1], back_recv.at[step - 1],
            "mem", source,
        )
        copy.start()
        backs.append(copy)
    back[tile] = back_own[...]
    for copy in outs:
        copy.wait_send()
    for copy in backs:
        copy.wait()
    image[...] = lax.dot_general(
        placing.astype(jnp.bfloat16), back[...].reshape(tiles * capacity, quarter),
        (((0,), (0,)), ((), ())), preferred_element_type=jnp.float32,
    )
    lane = lax.broadcasted_iota(jnp.int32, (patch, levels), 1)

    def gather_up(j, carry):
        own = jnp.broadcast_to(image[pl.ds(j, 1)], (levels, quarter)).astype(jnp.bfloat16)
        value = lax.dot_general(
            interp[j], own, (((1,), (1,)), ((), ())), preferred_element_type=jnp.float32
        )
        total = jnp.zeros((patch, levels), jnp.float32)
        for level in range(levels):
            total = jnp.where(lane == level, value[level * patch : (level + 1) * patch], total)
        spread[pl.ds(pl.multiple_of(j * patch, patch), patch)] = total
        return carry

    lax.fori_loop(0, blocks, gather_up, 0, unroll=4)
    high, low = split(spread[...])
    over = (((0,), (0,)), ((), ()))
    adj_parts[me] = lax.dot_general(
        high, select[...], over, preferred_element_type=jnp.float32
    ) + lax.dot_general(low, select[...], over, preferred_element_type=jnp.float32)
    sends = []
    for c, rows in enumerate(chunks):
        sends.append(spread_part(adj_parts, adj_send, adj_recv, c, rows, nband))
    local[...] = jnp.zeros_like(local)
    total = None
    for c in range(CHUNKS):
        for copy in sends[c]:
            copy.wait()
        for i in range(each):
            level = c * each + i
            adjoint = adj_parts[0, level : level + 1]
            for b in range(1, nband):
                adjoint = adjoint + adj_parts[b, level : level + 1]
            weighted = (all_ref[level].astype(jnp.float32) * adjoint).astype(jnp.bfloat16)
            term = lax.dot_general(
                weighted, eig_ref[level], (((1,), (1,)), ((), ())),
                preferred_element_type=jnp.float32,
            )
            total = term if total is None else total + term
    for b in range(nband):
        local[b, :, :modes_dev] = total[b * mem_dev : (b + 1) * mem_dev]
    copies = []
    for step in range(1, nband):
        peer = lax.rem(me + step, nband)
        copy = remote(
            local.at[peer], turned.at[me], turn_send.at[step - 1], turn_recv.at[step - 1],
            "band", peer,
        )
        copy.start()
        copies.append(copy)
    turned[me] = local[me]
    for copy in copies:
        copy.wait()
    own = turned[0]
    for b in range(1, nband):
        own = own + pltpu.roll(turned[b], b * modes_dev, 1)
    sums[tile] = own
    copies = []
    for step in range(1, tiles):
        peer = lax.rem(tile + step, tiles)
        copy = remote(
            sums.at[tile], sums.at[tile], sum_send.at[step - 1], sum_recv.at[step - 1],
            "mem", peer,
        )
        copy.start()
        copies.append(copy)
    for copy in copies:
        copy.wait()
    whole = sums[0]
    for t in range(1, tiles):
        whole = whole + sums[t]
    grad_ref[...] = control_ref[...] - scale * whole[:, : grad_ref.shape[1]]


def dma(*shape):
    return pltpu.SemaphoreType.DMA(shape)


def per_device(members, eigvecs, control, columns, interpolation, owners, innovation, obs_weight):
    nband = lax.axis_size("band")
    tiles = lax.axis_size("mem")
    band_idx = lax.axis_index("band")
    tile_idx = lax.axis_index("mem")
    mem_dev, levels, tile_cols = members.shape
    own_modes = eigvecs.shape[0]
    blocks, patch = columns.shape
    obs_block = interpolation.shape[2]
    capacity = innovation.shape[1] // tiles
    modes, total_members = control.shape
    scale = 1.0 / math.sqrt(modes * total_members)
    quarter = obs_block // nband
    eig_t = jnp.transpose(eigvecs, (1, 0, 2))
    mem_t = jnp.transpose(members, (1, 0, 2))
    weights = lax.dynamic_slice_in_dim(control, band_idx * own_modes, own_modes, 0)
    weights = weights.astype(jnp.bfloat16).T
    own_control = lax.dynamic_slice_in_dim(control, band_idx * mem_dev, mem_dev, 1)
    lanes = pl.cdiv(modes, 128) * 128
    slots = (tiles, capacity, quarter)
    own_slots = (1, tiles * capacity, quarter)
    hbm = pl.BlockSpec(memory_space=pltpu.HBM)
    f32, bf16 = jnp.float32, jnp.bfloat16
    gradient, departure = pl.pallas_call(
        functools.partial(whole_kernel, nband, tiles, scale),
        out_shape=(
            jax.ShapeDtypeStruct((mem_dev, modes), f32),
            jax.ShapeDtypeStruct(own_slots, f32),
        ),
        in_specs=[VMEM] * 6 + [hbm] * 3,
        out_specs=(VMEM, VMEM),
        scratch_shapes=[
            pltpu.VMEM((levels, total_members, tile_cols), bf16),
            pltpu.VMEM((levels, total_members, tile_cols), f32),
            pltpu.VMEM((nband, levels, tile_cols), f32),
            pltpu.VMEM((nband, levels, tile_cols), f32),
            pltpu.VMEM((blocks * patch, tile_cols), bf16),
            pltpu.VMEM((blocks, levels * patch, quarter), bf16),
            pltpu.VMEM(own_slots, f32),
            pltpu.VMEM(own_slots, f32),
            pltpu.VMEM((blocks, quarter), f32),
            pltpu.VMEM((blocks * patch, levels), f32),
            pltpu.VMEM(slots, f32),
            pltpu.VMEM(slots, f32),
            pltpu.VMEM(slots, bf16),
            pltpu.VMEM(slots, bf16),
            pltpu.VMEM((capacity, quarter), bf16),
            pltpu.VMEM((nband, mem_dev, lanes), f32),
            pltpu.VMEM((nband, mem_dev, lanes), f32),
            pltpu.VMEM((tiles, mem_dev, lanes), f32),
            dma(4), dma(), dma(), dma(CHUNKS), dma(CHUNKS), dma(CHUNKS), dma(CHUNKS),
            dma(CHUNKS, nband - 1), dma(CHUNKS, nband - 1),
            dma(tiles - 1), dma(tiles - 1), dma(tiles - 1), dma(tiles - 1),
            dma(CHUNKS, nband - 1), dma(CHUNKS, nband - 1),
            dma(nband - 1), dma(nband - 1), dma(tiles - 1), dma(tiles - 1),
        ],
        compiler_params=pltpu.CompilerParams(
            collective_id=1, has_side_effects=True, vmem_limit_bytes=40 << 20
        ),
    )(
        mem_t, eig_t, weights, columns.T, owners.reshape(tiles, blocks), own_control.T,
        *[pltpu.with_memory_space_constraint(x, pltpu.HBM) for x in (interpolation, innovation, obs_weight)],
    )
    return (gradient.T, departure)


def solution(mesh):
    return jax.shard_map(
        per_device,
        mesh=mesh,
        in_specs=(
            P("band", None, "mem"),
            P("band", None, "mem"),
            P(),
            P("mem", None),
            P("mem", None, None),
            P(),
            P("mem", None, None),
            P("mem", None, None),
        ),
        out_specs=(P(None, "band"), P("mem", None, "band")),
        check_vma=False,
    )
```
